32 devices in a mesh: gx: 4 (over y, x), gy: 4 (over z), gz: 2 (over core).
Axes of the slice: x: 2, y: 2, z: 4, core: 2. Of those that a mesh axis runs over, the one named last changes fastest.
Arguments:
- force: float32 [3, 128, 64, 256], P(None, 'gx', 'gy', 'gz'), may hold values from -6 to 6
- phase: int32 [128, 64, 256], P('gx', 'gy', 'gz'), may hold values from 0 to 7
- viscosity_table: float32 [8], replicated, may hold values from 0.1 to 10
- boundary_flags: int32 [6], replicated, may hold values from 0 to 1
Outputs:
- pressure: float32 [128, 64, 256], P('gx', 'gy', 'gz')
- residual: float32 [128, 64, 256], P('gx', 'gy', 'gz')
- res_norms: float32 [3], replicated
The draws below stay inside these ranges and needn't reach their ends.
Inputs may be any that keep to these rules, and one draw needn't show every extreme that they name: phase ids index viscosity_table. `boundary_flags`: 0 marks a no-slip face, 1 a free-slip face.
All inputs are finite; a program needn't handle non-finite values.
Results may differ from the reference program's by a relative error of at most 0.0003.
Values sent between devices are 32-bit elements; how exact they have to be, the bound alone decides.
A program may use at most 192 MiB of HBM per device.

```python
import math
import jax
import jax.numpy as jnp
from jax import lax

ITERS = 3
SWEEPS = 4
PHASES = 8
NX = 128
NY = 64
NZ = 256


def touch_ends(values, stream_key, low, high):
    dims = values.shape
    spot = [jax.random.randint(jax.random.fold_in(stream_key, axis), (), 0, dims[axis]) for axis in range(len(dims))]
    values = values.at[tuple(spot)].set(low)
    longest = dims.index(max(dims))
    spot[longest] = (spot[longest] + 1) % dims[longest]
    return values.at[tuple(spot)].set(high)


def level_of(own_key, shape, pieces, low, largest):
    gain, own = 1.0, jax.random.fold_in(own_key, 6)
    for axis_at, blocks in pieces:
        heights = jnp.exp(jax.random.uniform(jax.random.fold_in(own, axis_at), (blocks,), jnp.float32, low / len(pieces), largest / len(pieces)))
        gain = gain * jnp.repeat(heights, shape[axis_at] // blocks).reshape([-1 if axis == axis_at else 1 for axis in range(len(shape))])
    return gain


def normal_values(stream_key, dims, spread, reach, shards=(), kind=jnp.bfloat16):
    values = jax.random.normal(stream_key, dims, jnp.float32) * spread
    if len(shards) > 0:
        values = level_of(stream_key, dims, shards, -0.22, 0.18) * values
    return jnp.clip(values, min=-reach, max=reach).astype(kind)


def setup_inputs(seed: int = 0) -> dict:
    splits = jax.random.split(jax.random.key(seed), 5)
    force = normal_values(splits[0], (3, NX, NY, NZ), 1.0, 6.0, ((1, 4), (2, 4), (3, 2)), jnp.float32)
    phase = touch_ends(jax.random.randint(splits[1], (NX, NY, NZ), 0, PHASES), jax.random.fold_in(splits[1], 1), 0, PHASES - 1).astype(jnp.int32)
    viscosity_table = jnp.clip(jnp.exp(jax.random.uniform(splits[2], (PHASES,), jnp.float32, math.log(0.1), math.log(10.0))), 0.1, 10.0)
    boundary_flags = touch_ends(jax.random.randint(splits[3], (6,), 0, 2), jax.random.fold_in(splits[3], 1), 0, 1).astype(jnp.int32)
    return dict(force=force, phase=phase, viscosity_table=viscosity_table, boundary_flags=boundary_flags)


OMEGA = 0.8


def lookup(phase, table):
    eta = jnp.zeros(phase.shape, jnp.float32)
    for level in range(table.shape[0]):
        eta = eta + jnp.where(phase == level, table[level], jnp.float32(0.0))
    return eta


def trim(array, keep):
    for dim in range(3):
        if dim != keep:
            array = lax.slice_in_dim(array, 1, array.shape[dim] - 1, axis=dim)
    return array


def coefficients(eta_wide, flags, starts, totals):
    walls = (flags == 0).astype(jnp.float32)
    inner = eta_wide[1:-1, 1:-1, 1:-1]
    faces = []
    diag = [jnp.zeros_like(inner) for comp in range(3)]
    for axis in range(3):
        length = eta_wide.shape[axis]
        spots = starts[axis] + jnp.arange(length, dtype=jnp.int32)
        inside = (spots >= 0) & (spots < totals[axis])
        shape = [1, 1, 1]
        shape[axis] = length - 2
        upper_in = inside[2:].reshape(shape)
        lower_in = inside[:-2].reshape(shape)
        sides = trim(eta_wide, axis)
        middle = lax.slice_in_dim(sides, 1, length - 1, axis=axis)
        upper = 0.5 * (middle + lax.slice_in_dim(sides, 2, length, axis=axis))
        lower = 0.5 * (middle + lax.slice_in_dim(sides, 0, length - 2, axis=axis))
        faces.append((jnp.where(upper_in, upper, 0.0), jnp.where(lower_in, lower, 0.0)))
        for comp in range(3):
            normal = 1.0 if comp == axis else 0.0
            wall_low = jnp.maximum(walls[2 * axis], normal)
            wall_high = jnp.maximum(walls[2 * axis + 1], normal)
            diag[comp] = diag[comp] + jnp.where(upper_in, upper, wall_high * inner) + jnp.where(lower_in, lower, wall_low * inner)
    return faces, jnp.stack(diag)


def viscous(wide, faces, diag):
    result = diag * wide[:, 1:-1, 1:-1, 1:-1]
    for axis in range(3):
        dim = axis + 1
        sides = wide
        for other in range(1, 4):
            if other != dim:
                sides = lax.slice_in_dim(sides, 1, sides.shape[other] - 1, axis=other)
        length = wide.shape[dim]
        result = result - faces[axis][0] * lax.slice_in_dim(sides, 2, length, axis=dim)
        result = result - faces[axis][1] * lax.slice_in_dim(sides, 0, length - 2, axis=dim)
    return result


def smooth(source, faces, diag, inverse):
    state = OMEGA * inverse * source
    for sweep in range(SWEEPS - 1):
        wide = jnp.pad(state, ((0, 0), (1, 1), (1, 1), (1, 1)))
        state = state + OMEGA * inverse * (source - viscous(wide, faces, diag))
    return state


def gradient(field):
    padded = jnp.pad(field, ((0, 1), (0, 1), (0, 1)))
    return jnp.stack([padded[1:, :-1, :-1] - field, padded[:-1, 1:, :-1] - field, padded[:-1, :-1, 1:] - field])


def divergence(velocity):
    total = jnp.zeros(velocity.shape[1:], jnp.float32)
    for axis in range(3):
        comp = velocity[axis]
        widths = [(0, 0), (0, 0), (0, 0)]
        widths[axis] = (1, 0)
        before = lax.slice_in_dim(jnp.pad(comp, widths), 0, comp.shape[axis], axis=axis)
        total = total + before - comp
    return total


def reference(force, phase, viscosity_table, boundary_flags):
    eta = lookup(phase, viscosity_table)
    faces, diag = coefficients(jnp.pad(eta, 1), boundary_flags, (-1, -1, -1), (NX, NY, NZ))
    inverse = 1.0 / diag

    def schur(field):
        return divergence(smooth(gradient(field), faces, diag, inverse))

    rhs = divergence(smooth(force, faces, diag, inverse))
    cells = float(NX * NY * NZ)
    pressure = jnp.zeros_like(rhs)
    residual = rhs
    scaled = eta * residual
    search = scaled
    gamma = jnp.sum(residual * scaled)
    squares = jnp.sum(residual * residual)
    norms = []
    for step in range(ITERS):
        norms.append(squares / cells)
        image = schur(search)
        alpha = gamma / jnp.sum(search * image)
        pressure = pressure + alpha * search
        residual = residual - alpha * image
        if step + 1 < ITERS:
            scaled = eta * residual
            gamma_new = jnp.sum(residual * scaled)
            squares = jnp.sum(residual * residual)
            search = scaled + (gamma_new / gamma) * search
            gamma = gamma_new
    return pressure, residual, jnp.stack(norms)
```

```python
import jax
import jax.numpy as jnp
from jax import lax
from jax.sharding import PartitionSpec as P

ITERS = 3
SWEEPS = 4


OMEGA = 0.8


def passed_along(value, axis, by):
    devices = lax.axis_size(axis)
    pairs = [(i, i + by) for i in range(devices) if 0 <= i + by < devices]
    return lax.ppermute(value, axis, pairs)


def extended(cells, sides, width):
    for axis, dim in sides:
        count = lax.axis_size(axis)
        ends = count - 1
        head = lax.slice_in_dim(cells, 0, width, axis=dim)
        tail = lax.slice_in_dim(cells, cells.shape[dim] - width, cells.shape[dim], axis=dim)
        cells = jnp.concatenate(
            [
                lax.ppermute(tail, axis, [(i, (i + 1) % count) for i in range(ends)]),
                cells,
                lax.ppermute(head, axis, [((i + 1) % count, i) for i in range(ends)]),
            ],
            axis=dim,
        )
    return cells


def lookup(phase, table):
    eta = jnp.zeros(phase.shape, jnp.float32)
    for level in range(table.shape[0]):
        eta = eta + jnp.where(phase == level, table[level], jnp.float32(0.0))
    return eta


def trim(array, keep):
    for dim in range(3):
        if dim != keep:
            array = lax.slice_in_dim(array, 1, array.shape[dim] - 1, axis=dim)
    return array


def coefficients(eta_wide, flags, starts, totals):
    walls = (flags == 0).astype(jnp.float32)
    inner = eta_wide[1:-1, 1:-1, 1:-1]
    faces = []
    diag = [jnp.zeros_like(inner) for comp in range(3)]
    for axis in range(3):
        length = eta_wide.shape[axis]
        spots = starts[axis] + jnp.arange(length, dtype=jnp.int32)
        inside = (spots >= 0) & (spots < totals[axis])
        shape = [1, 1, 1]
        shape[axis] = length - 2
        upper_in = inside[2:].reshape(shape)
        lower_in = inside[:-2].reshape(shape)
        sides = trim(eta_wide, axis)
        middle = lax.slice_in_dim(sides, 1, length - 1, axis=axis)
        upper = 0.5 * (middle + lax.slice_in_dim(sides, 2, length, axis=axis))
        lower = 0.5 * (middle + lax.slice_in_dim(sides, 0, length - 2, axis=axis))
        faces.append((jnp.where(upper_in, upper, 0.0), jnp.where(lower_in, lower, 0.0)))
        for comp in range(3):
            normal = 1.0 if comp == axis else 0.0
            wall_low = jnp.maximum(walls[2 * axis], normal)
            wall_high = jnp.maximum(walls[2 * axis + 1], normal)
            diag[comp] = (
                diag[comp]
                + jnp.where(upper_in, upper, wall_high * inner)
                + jnp.where(lower_in, lower, wall_low * inner)
            )
    return (faces, jnp.stack(diag))


def viscous(state, faces, diag):
    ends = []
    for axis, name in enumerate(("gx", "gy", "gz")):
        dim = axis + 1
        length = state.shape[dim]
        head = lax.slice_in_dim(state, 0, 1, axis=dim)
        tail = lax.slice_in_dim(state, length - 1, length, axis=dim)
        ends.append((passed_along(head, name, -1), passed_along(tail, name, 1)))
    result = diag * state
    for axis in range(3):
        dim = axis + 1
        length = state.shape[dim]
        above, below = ends[axis]
        upper = jnp.concatenate([lax.slice_in_dim(state, 1, length, axis=dim), above], dim)
        lower = jnp.concatenate([below, lax.slice_in_dim(state, 0, length - 1, axis=dim)], dim)
        result = result - faces[axis][0] * upper
        result = result - faces[axis][1] * lower
    return result


def gradient(field):
    upper_x = passed_along(field[0:1], "gx", -1)
    upper_y = passed_along(field[:, 0:1], "gy", -1)
    upper_z = passed_along(field[:, :, 0:1], "gz", -1)
    along_x = jnp.concatenate([field[1:], upper_x], 0) - field
    along_y = jnp.concatenate([field[:, 1:], upper_y], 1) - field
    along_z = jnp.concatenate([field[:, :, 1:], upper_z], 2) - field
    return jnp.stack([along_x, along_y, along_z])


def divergence(velocity):
    lower_x = passed_along(velocity[0][-1:], "gx", 1)
    lower_y = passed_along(velocity[1][:, -1:], "gy", 1)
    lower_z = passed_along(velocity[2][:, :, -1:], "gz", 1)
    total = jnp.concatenate([lower_x, velocity[0][:-1]], 0) - velocity[0]
    total = total + jnp.concatenate([lower_y, velocity[1][:, :-1]], 1) - velocity[1]
    total = total + jnp.concatenate([lower_z, velocity[2][:, :, :-1]], 2) - velocity[2]
    return total


def per_device(force, phase, viscosity_table, boundary_flags):
    rows = phase.shape
    totals = (
        rows[0] * lax.axis_size("gx"),
        rows[1] * lax.axis_size("gy"),
        rows[2] * lax.axis_size("gz"),
    )
    indices = (lax.axis_index("gx"), lax.axis_index("gy"), lax.axis_index("gz"))
    cells = float(totals[0] * totals[1] * totals[2])
    phase_wide = extended(phase, (("gx", 0), ("gy", 1), ("gz", 2)), 1)
    starts = tuple((indices[dim] * rows[dim] - 1 for dim in range(3)))
    eta_wide = lookup(phase_wide, viscosity_table)
    faces, diag = coefficients(eta_wide, boundary_flags, starts, totals)
    eta = eta_wide[1:-1, 1:-1, 1:-1]
    inverse = 1.0 / diag

    def sweeps(source, state, count):
        for sweep in range(count):
            state = state + OMEGA * inverse * (source - viscous(state, faces, diag))
        return state

    def schur(field):
        source = gradient(field)
        return divergence(sweeps(source, OMEGA * inverse * source, SWEEPS - 1))

    rhs = divergence(sweeps(force, OMEGA * inverse * force, SWEEPS - 1))
    pressure = jnp.zeros_like(rhs)
    residual = rhs
    norms = []
    scaled = eta * residual
    applied = schur(scaled)
    for step in range(ITERS):
        last = step + 1 == ITERS
        gamma, delta, squares = lax.psum(
            (jnp.sum(residual * scaled), jnp.sum(applied * scaled), jnp.sum(residual * residual)),
            ("gx", "gy", "gz"),
        )
        norms.append(squares / cells)
        if not last:
            mass_applied = eta * applied
            twice_applied = schur(mass_applied)
        if step == 0:
            alpha = gamma / delta
            search = scaled
            search_image = applied
            scaled_image = mass_applied
            applied_image = twice_applied
        else:
            beta = gamma / gamma_old
            alpha = gamma / (delta - beta * gamma / alpha_old)
            search = scaled + beta * search
            search_image = applied + beta * search_image
            if not last:
                scaled_image = mass_applied + beta * scaled_image
                applied_image = twice_applied + beta * applied_image
        pressure = pressure + alpha * search
        residual = residual - alpha * search_image
        if not last:
            scaled = scaled - alpha * scaled_image
            applied = applied - alpha * applied_image
        gamma_old = gamma
        alpha_old = alpha
    return (pressure, residual, jnp.stack(norms))


def solution(mesh):
    placed = (P(None, "gx", "gy", "gz"), P("gx", "gy", "gz"), P(), P())
    return jax.shard_map(
        per_device,
        mesh=mesh,
        in_specs=placed,
        out_specs=(P("gx", "gy", "gz"), P("gx", "gy", "gz"), P()),
        check_vma=False,
    )
```
